128 devices in a mesh: section: 4 (over z_hi, core), lane: 32 (over x, y, z_lo).
Axes of the slice: x: 4, y: 4, z: 4 (z_hi: 2, z_lo: 2; z = z_hi * 2 + z_lo), core: 2. Of those that a mesh axis runs over, the one named last changes fastest.
Arguments:
- voltages: bfloat16 [2, 2048, 49152], P(None, ('section', 'lane')), may hold values from -6 to 6
- earlier_covariance: bfloat16 [128, 2, 2048, 2048], P(('section', 'lane')), may hold values from -0.25 to 16, as said below
- antenna_pos: int32 [2048], replicated, may hold values from 0 to 4095
- beam_dir: int32 [128], replicated, may hold values from 0 to 4095
Outputs:
- timeseries: float32 [128, 2, 49152], P(('section', 'lane'))
The draws below stay inside these ranges and needn't reach their ends.
Inputs may be any that keep to these rules, and one draw needn't show every extreme that they name: `earlier_covariance`: each channel's matrix is Hermitian: part 0 symmetric, part 1 antisymmetric with zero diagonal, and positive definite.
All inputs are finite; a program needn't handle non-finite values.
Results may differ from the reference program's by a relative error of at most 0.0075.
Values may be sent and summed in bfloat16 or wider, within the bound.
No kernel may reach another device: no remote copies, remote signals or barrier semaphores. Data moves between devices by JAX's collectives and lax.ppermute only.
A program may use at most 192 MiB of HBM per device.

```python
import math
import jax
import jax.numpy as jnp
from jax import lax

ANTENNAS = 2048
FREQUENCY_BINS = 128
BEAMS = 128
SPECTRA = 384
CHEB = 2
LOAD_PCT = 10
KEEP_PCT = 50


def draw_earlier_covariance(key, part):

    def one_channel(channel):
        subkey = jax.random.fold_in(key, channel)
        noise = jax.random.normal(jax.random.fold_in(subkey, 11), (2, ANTENNAS, ANTENNAS), jnp.float32)
        spread = 1.5 / (2.0 * jnp.sqrt(2.0 * ANTENNAS))
        real_part = (noise[0] + noise[0].T) * (spread / jnp.sqrt(2.0))
        imag_part = (noise[1] - noise[1].T) * (spread / jnp.sqrt(2.0))
        low_end, high_end = (2.0, 5.0)
        diagonal = jnp.exp(jax.random.uniform(jax.random.fold_in(subkey, 23), (ANTENNAS,), jnp.float32, jnp.log(low_end), jnp.log(high_end)))
        identity = jnp.eye(ANTENNAS, dtype=bool)
        real_part = jnp.where(identity, diagonal[None, :], real_part)
        return jnp.stack([real_part, imag_part], axis=0).astype(jnp.bfloat16)
    return lax.map(one_channel, jnp.arange(FREQUENCY_BINS, dtype=jnp.int32))


def set_ends(result, stream_key, smallest, top_value):
    longest = result.shape.index(max(result.shape))
    spots = []
    for shift in (0, 1):
        where = [jax.random.randint(jax.random.fold_in(stream_key, axis), (), 0, length) for axis, length in enumerate(result.shape)]
        where[longest] = (where[longest] + shift) % result.shape[longest]
        spots.append(tuple(where))
    return result.at[spots[0]].set(smallest).at[spots[1]].set(top_value)


def level_of(key, extent, cuts, smallest, top_value):
    factor_of = 1.0
    for axis_at, shards_of in cuts:
        steps = jax.random.uniform(jax.random.fold_in(jax.random.fold_in(key, 6), axis_at), (shards_of,), jnp.float32, smallest / len(cuts), top_value / len(cuts))
        factor_of = factor_of * jnp.repeat(jnp.exp(steps), extent[axis_at] // shards_of).reshape((-1,) + (1,) * (len(extent) - 1 - axis_at))
    return factor_of


def scatter_about(stream_key, shape, scale, reach, pieces=(), kind=jnp.bfloat16):
    factor_of = level_of(stream_key, shape, pieces, -0.22, 0.18) if pieces else 1.0
    drawn = jax.random.normal(stream_key, shape, jnp.float32) * scale * factor_of
    return jnp.minimum(jnp.maximum(drawn, -reach), reach).astype(kind)


def setup_inputs(seed: int = 0) -> dict:
    arg_keys = jax.random.split(jax.random.key(seed), 5)
    return {
        "voltages": scatter_about(arg_keys[0], (2, ANTENNAS, SPECTRA * FREQUENCY_BINS), 1.0, 6.0, ((1, 128),)),
        "earlier_covariance": draw_earlier_covariance(jax.random.fold_in(arg_keys[4], 71), 0),
        "antenna_pos": set_ends(jax.random.randint(arg_keys[2], (ANTENNAS,), 0, 4096), jax.random.fold_in(arg_keys[2], 1), 0, 4095).astype(jnp.int32),
        "beam_dir": set_ends(jax.random.randint(arg_keys[3], (BEAMS,), 0, 4096), jax.random.fold_in(arg_keys[3], 1), 0, 4095).astype(jnp.int32),
    }


phase_steps = 4096

def fourier_matrix(length, sign):
    counter = jnp.arange(length, dtype=jnp.int32)
    angle = (counter[:, None] * counter[None, :] % length).astype(jnp.float32) * (2.0 * math.pi / length)
    cosine = jnp.cos(angle) / math.sqrt(length)
    sine = sign * jnp.sin(angle) / math.sqrt(length)
    return jnp.stack([jnp.stack([cosine, sine], axis=1), jnp.stack([-sine, cosine], axis=1)], axis=0).astype(jnp.bfloat16)

def apply_matrix(cov_real, cov_imag, loading, vector):
    half = vector.shape[1] // 2
    high = lax.Precision.HIGHEST
    with_real = jnp.dot(cov_real, vector, precision=high, preferred_element_type=jnp.float32)
    with_imag = jnp.dot(cov_imag, vector, precision=high, preferred_element_type=jnp.float32)
    out_real = with_real[:, :half] - with_imag[:, half:] + loading * vector[:, :half]
    out_imag = with_imag[:, :half] + with_real[:, half:] + loading * vector[:, half:]
    return jnp.concatenate([out_real, out_imag], axis=1)

def compute_beam_weights(spectrum, prior, channel, antenna_pos, beam_dir):
    voltage_samples = spectrum.shape[-1]
    antennas = spectrum.shape[1]
    stacked = jnp.concatenate([spectrum[0], spectrum[1]], axis=1)
    rotated = jnp.concatenate([spectrum[1], -spectrum[0]], axis=1)
    data_real = jnp.dot(stacked, stacked.T, preferred_element_type=jnp.float32)
    data_imag = jnp.dot(rotated, stacked.T, preferred_element_type=jnp.float32)
    keep = KEEP_PCT / 100.0
    cov_real = keep * prior[0].astype(jnp.float32) + (1.0 - keep) / voltage_samples * data_real
    cov_imag = keep * prior[1].astype(jnp.float32) + (1.0 - keep) / voltage_samples * data_imag
    mean_diag = jnp.trace(cov_real) / antennas
    loading = LOAD_PCT / 100.0 * mean_diag
    upper = 5.0 * mean_diag
    phase_int = antenna_pos[:, None] * beam_dir[None, :] % phase_steps * (channel + FREQUENCY_BINS) % phase_steps
    angle = phase_int.astype(jnp.float32) * (2.0 * math.pi / phase_steps)
    remain = jnp.concatenate([jnp.cos(angle), jnp.sin(angle)], axis=1)
    center = 0.5 * (upper + loading)
    radius = 0.5 * (upper - loading)
    ratio = center / radius
    factor = 1.0 / ratio
    iterate = jnp.zeros_like(remain)
    update = remain / center
    for step in range(CHEB):
        iterate = iterate + update
        if step + 1 < CHEB:
            remain = remain - apply_matrix(cov_real, cov_imag, loading, update)
            factor_next = 1.0 / (2.0 * ratio - factor)
            update = factor_next * factor * update + 2.0 * factor_next / radius * remain
            factor = factor_next
    half = iterate.shape[1] // 2
    return jnp.stack([iterate[:, :half], iterate[:, half:]], axis=0).astype(jnp.bfloat16)

def project(beam_weight_set, spectra):
    rotated = jnp.stack([spectra, jnp.stack([spectra[:, 1], -spectra[:, 0]], axis=1)], axis=1)
    return jnp.einsum('npab,nqpas->nqbs', beam_weight_set.astype(jnp.float32), rotated.astype(jnp.float32))

def reference(voltages, earlier_covariance, antenna_pos, beam_dir):
    tapered_signal = voltages.reshape(2, ANTENNAS, SPECTRA, FREQUENCY_BINS)
    forward = fourier_matrix(FREQUENCY_BINS, -1.0).astype(jnp.float32)
    spectra = jnp.einsum('past,ptqk->kqas', tapered_signal.astype(jnp.float32), forward).astype(jnp.bfloat16)

    def solve_item(item):
        return compute_beam_weights(item[0], item[1], item[2], antenna_pos, beam_dir)
    channel_ids = jnp.arange(FREQUENCY_BINS, dtype=jnp.int32)
    beam_weight_set = lax.map(solve_item, (spectra, earlier_covariance, channel_ids))
    padded = jnp.pad(beam_weight_set, ((1, 1), (0, 0), (0, 0), (0, 0)))

    def beam_item(item):
        lower_w, own_w, upper_w, spectrum = item
        spectrum = spectrum[None]
        total = project(lower_w[None], spectrum) + 2.0 * project(own_w[None], spectrum) + project(upper_w[None], spectrum)
        return (0.25 * total[0]).astype(jnp.bfloat16)
    beamed = lax.map(beam_item, (padded[:-2], padded[1:-1], padded[2:], spectra))
    inverse = fourier_matrix(FREQUENCY_BINS, 1.0).astype(jnp.float32)
    series = jnp.einsum('kpbs,pkqt->bqst', beamed.astype(jnp.float32), inverse)
    return series.reshape(BEAMS, 2, SPECTRA * FREQUENCY_BINS)
```

```python
import math

import jax
import jax.numpy as jnp
import ml_dtypes
import numpy as np
from jax import lax
from jax.experimental import pallas as pl
from jax.experimental.pallas import tpu as pltpu
from jax.sharding import Mesh
from jax.sharding import PartitionSpec as P

FREQUENCY_BINS = 128
LOAD_PCT = 10
KEEP_PCT = 50
PHASE_STEPS = 4096

PARTS = ("zh", "core", "x", "y", "zl")
SIZES = (2, 2, 4, 4, 2)
SOLVER = ("zh", "zl", "x", "y", "core")
DEVICES = 128

ANTENNAS = 2048
BEAMS = 128
SPECTRA = 384
HERE = 16
CHUNK = 512
COLUMNS = 256

BF = jnp.bfloat16
F32 = jnp.float32
ANY = pl.BlockSpec(memory_space=pl.ANY)
SMEM = pl.BlockSpec(memory_space=pltpu.SMEM)


def solver_index():
    grid = np.arange(DEVICES).reshape(SIZES)
    return np.transpose(grid, (0, 4, 2, 3, 1)).reshape(-1)


def fourier_matrix(length, sign):
    counter = np.arange(length, dtype=np.int64)
    angle = (counter[:, None] * counter[None, :] % length) * (2.0 * math.pi / length)
    cosine = np.cos(angle) / math.sqrt(length)
    sine = sign * np.sin(angle) / math.sqrt(length)
    table = np.stack([np.stack([cosine, sine], axis=1), np.stack([-sine, cosine], axis=1)], axis=0)
    return table.astype(np.float32).astype(ml_dtypes.bfloat16)


def dot(a, b):
    return jnp.dot(a, b, preferred_element_type=F32)


def steering(pos, directions, channel):
    phase = ((pos * directions) & (PHASE_STEPS - 1)) * (channel + FREQUENCY_BINS)
    moved = (phase & (PHASE_STEPS - 1)) + 512
    quadrant = moved >> 10
    x = ((moved & 1023) - 512).astype(F32) * (2.0 * math.pi / PHASE_STEPS)
    y = x * x
    sine = 1.0 / 362880.0
    for c in (-1.0 / 5040.0, 1.0 / 120.0, -1.0 / 6.0, 1.0):
        sine = sine * y + c
    sine = sine * x
    cosine = 1.0 / 40320.0
    for c in (-1.0 / 720.0, 1.0 / 24.0, -0.5, 1.0):
        cosine = cosine * y + c
    odd = (quadrant & 1) == 1
    c = jnp.where(odd, sine, cosine)
    s = jnp.where(odd, cosine, sine)
    c = jnp.where(((quadrant + 1) & 2) == 2, -c, c)
    s = jnp.where((quadrant & 2) == 2, -s, s)
    return c, s


def earlier_kernel(channels, pos, directions, earlier, product, trace, steer, coarse, own):
    j = pl.program_id(0)

    @pl.when(j == 0)
    def _():
        trace[...] = jnp.zeros_like(trace)
        for i in range(ANTENNAS // COLUMNS):
            at = slice(i * COLUMNS, (i + 1) * COLUMNS)
            c, s = steering(pos[:, at], directions[...], channels[0])
            own[:BEAMS, at] = c.astype(BF)
            own[BEAMS:, at] = s.astype(BF)

    here = pl.ds(pl.multiple_of(j * COLUMNS, COLUMNS), COLUMNS)
    c, s = steering(pos[:, here], directions[...], channels[1])
    steer[:BEAMS] = c
    steer[BEAMS:] = s
    coarse[:BEAMS] = c.astype(BF)
    coarse[BEAMS:] = s.astype(BF)
    first = dot(own[...], earlier[0, 0])
    second = dot(own[...], earlier[0, 1])
    product[:BEAMS] = (first[:BEAMS] + second[BEAMS:]).astype(BF)
    product[BEAMS:] = (first[BEAMS:] - second[:BEAMS]).astype(BF)
    square = earlier[0, 0, here, :].astype(F32)
    row = lax.broadcasted_iota(jnp.int32, square.shape, 0)
    column = lax.broadcasted_iota(jnp.int32, square.shape, 1)
    kept = jnp.where(row == column, square, 0.0)
    kept = jnp.sum(kept.reshape(COLUMNS // 8, 8, COLUMNS), axis=0)
    trace[...] += kept[:, :128] + kept[:, 128:]


def earlier_product(channels, pos, directions, earlier):
    steps = ANTENNAS // COLUMNS
    wide = pl.BlockSpec((2 * BEAMS, COLUMNS), lambda j: (0, j))
    return pl.pallas_call(
        earlier_kernel,
        grid=(steps,),
        in_specs=[
            SMEM,
            pl.BlockSpec((1, ANTENNAS), lambda j: (0, 0)),
            pl.BlockSpec((BEAMS, 1), lambda j: (0, 0)),
            pl.BlockSpec((1, 2, ANTENNAS, COLUMNS), lambda j: (0, 0, 0, j)),
        ],
        out_specs=[wide, pl.BlockSpec((8, 128), lambda j: (0, 0)), wide, wide],
        out_shape=[
            jax.ShapeDtypeStruct((2 * BEAMS, ANTENNAS), BF),
            jax.ShapeDtypeStruct((8, 128), F32),
            jax.ShapeDtypeStruct((2 * BEAMS, ANTENNAS), F32),
            jax.ShapeDtypeStruct((2 * BEAMS, ANTENNAS), BF),
        ],
        scratch_shapes=[pltpu.VMEM((2 * BEAMS, ANTENNAS), BF)],
        name="earlier_product",
    )(channels, pos, directions, earlier)


def chunk_copies(here, held, sems, chunk):
    zh, core = divmod(chunk, 2)
    out = []
    for zl in range(2):
        for q in range(2):
            out.append(
                pltpu.make_async_copy(
                    here.at[zh, zl, :, :, core, q],
                    held.at[q, chunk, :, :, zl],
                    sems.at[chunk * 4 + zl * 2 + q],
                )
            )
    return out


HELD = pltpu.VMEM((2, 4, 4, 4, 2, HERE, SPECTRA), BF)


def weights_kernel(here, steer, coarse, product, trace, out, held, steer_v, coarse_v, product_v, sems, more):
    extra = [
        pltpu.make_async_copy(coarse, coarse_v, more.at[0]),
        pltpu.make_async_copy(product, product_v, more.at[1]),
        pltpu.make_async_copy(steer, steer_v, more.at[2]),
    ]
    extra[0].start()
    copies = [chunk_copies(here, held, sems, chunk) for chunk in range(4)]
    for group in copies:
        for c in group:
            c.start()
    extra[1].start()
    extra[2].start()
    extra[0].wait()

    first = jnp.zeros((2 * BEAMS, SPECTRA), F32)
    second = jnp.zeros((2 * BEAMS, SPECTRA), F32)
    power = jnp.zeros((8, SPECTRA), F32)
    for chunk in range(4):
        for c in copies[chunk]:
            c.wait()
        at = slice(chunk * CHUNK, (chunk + 1) * CHUNK)
        xr = held[0, chunk].reshape(CHUNK, SPECTRA)
        xi = held[1, chunk].reshape(CHUNK, SPECTRA)
        first += dot(coarse_v[:, at], xr)
        second += dot(coarse_v[:, at], xi)
        for x in (xr, xi):
            x = x.astype(F32).reshape(CHUNK // 8, 8, SPECTRA)
            power += jnp.sum(x * x, axis=0)
    inner = jnp.concatenate(
        [first[:BEAMS] + second[BEAMS:], first[BEAMS:] - second[:BEAMS]], axis=0
    ).astype(BF)

    keep = KEEP_PCT / 100.0
    fresh = (1.0 - keep) / SPECTRA
    total = jnp.sum(power, keepdims=True) * fresh + jnp.sum(trace[...], keepdims=True) * keep
    mean_diag = total * (1.0 / ANTENNAS)
    loading = LOAD_PCT / 100.0 * mean_diag
    upper = 5.0 * mean_diag
    center = 0.5 * (upper + loading)
    radius = 0.5 * (upper - loading)
    ratio = center / radius
    factor = 1.0 / ratio
    factor_next = 1.0 / (2.0 * ratio - factor)
    beta = 2.0 * factor_next / (radius * center)
    alpha = (1.0 + factor_next * factor) / center + 2.0 * factor_next / radius
    by_steer = alpha - beta * loading
    by_product = -keep * beta
    by_data = -fresh * beta

    extra[1].wait()
    extra[2].wait()
    turned = (((1,), (1,)), ((), ()))
    for chunk in range(4):
        at = slice(chunk * CHUNK, (chunk + 1) * CHUNK)
        xr = held[0, chunk].reshape(CHUNK, SPECTRA)
        xi = held[1, chunk].reshape(CHUNK, SPECTRA)
        p = lax.dot_general(inner, xr, turned, preferred_element_type=F32)
        q = lax.dot_general(inner, xi, turned, preferred_element_type=F32)
        for half, data in ((0, p[:BEAMS] - q[BEAMS:]), (1, p[BEAMS:] + q[:BEAMS])):
            rows = slice(half * BEAMS, (half + 1) * BEAMS)
            out[rows, at] = (
                by_steer * steer_v[rows, at]
                + by_product * product_v[rows, at].astype(F32)
                + by_data * data
            ).astype(BF)


def solve(here, steer, coarse, product, trace):
    return pl.pallas_call(
        weights_kernel,
        in_specs=[ANY, ANY, ANY, ANY, pl.BlockSpec(memory_space=pltpu.VMEM)],
        out_specs=pl.BlockSpec(memory_space=pltpu.VMEM),
        out_shape=jax.ShapeDtypeStruct((2 * BEAMS, ANTENNAS), BF),
        scratch_shapes=[
            HELD,
            pltpu.VMEM((2 * BEAMS, ANTENNAS), F32),
            pltpu.VMEM((2 * BEAMS, ANTENNAS), BF),
            pltpu.VMEM((2 * BEAMS, ANTENNAS), BF),
            pltpu.SemaphoreType.DMA((16,)),
            pltpu.SemaphoreType.DMA((3,)),
        ],
        name="weights",
    )(here, steer, coarse, product, trace)


def beams_kernel(here, lower, own, higher, out, held, sides, sems, more):
    copies = [chunk_copies(here, held, sems, chunk) for chunk in range(4)]
    parts = []
    for chunk in range(4):
        at = pl.ds(chunk * CHUNK, CHUNK)
        parts.append(
            [
                pltpu.make_async_copy(w.at[:, at], sides.at[i, :, at], more.at[chunk * 3 + i])
                for i, w in enumerate((lower, own, higher))
            ]
        )
        for c in parts[chunk] + copies[chunk]:
            c.start()
    first = jnp.zeros((2 * BEAMS, SPECTRA), F32)
    second = jnp.zeros((2 * BEAMS, SPECTRA), F32)
    for chunk in range(4):
        for c in parts[chunk] + copies[chunk]:
            c.wait()
        at = slice(chunk * CHUNK, (chunk + 1) * CHUNK)
        smooth = (
            0.25 * (sides[0, :, at].astype(F32) + sides[2, :, at].astype(F32))
            + 0.5 * sides[1, :, at].astype(F32)
        ).astype(BF)
        first += dot(smooth, held[0, chunk].reshape(CHUNK, SPECTRA))
        second += dot(smooth, held[1, chunk].reshape(CHUNK, SPECTRA))
    out[0] = (first[:BEAMS] + second[BEAMS:]).astype(BF)
    out[1] = (second[:BEAMS] - first[BEAMS:]).astype(BF)


def form_beams(here, lower, own, higher):
    return pl.pallas_call(
        beams_kernel,
        in_specs=[ANY, ANY, ANY, ANY],
        out_specs=pl.BlockSpec(memory_space=pltpu.VMEM),
        out_shape=jax.ShapeDtypeStruct((2, BEAMS, SPECTRA), BF),
        scratch_shapes=[
            HELD,
            pltpu.VMEM((3, 2 * BEAMS, ANTENNAS), BF),
            pltpu.SemaphoreType.DMA((16,)),
            pltpu.SemaphoreType.DMA((12,)),
        ],
        name="form_beams",
    )(here, lower, own, higher)


def shards(voltages, earlier, antenna_pos, beam_dir):
    signal = voltages.reshape(2, HERE, SPECTRA, FREQUENCY_BINS)
    spectra = jnp.einsum(
        "ptqk,past->kqas", fourier_matrix(FREQUENCY_BINS, -1.0), signal, preferred_element_type=F32
    ).astype(BF)
    here = lax.all_to_all(spectra, SOLVER, split_axis=0, concat_axis=0, tiled=True)
    here = here.reshape(2, 2, 4, 4, 2, 2, HERE, SPECTRA)

    channels = jnp.stack([lax.axis_index(PARTS), lax.axis_index(SOLVER)]).astype(jnp.int32)
    product, trace, steer, coarse = earlier_product(
        channels, antenna_pos.reshape(1, ANTENNAS), beam_dir.reshape(BEAMS, 1), earlier
    )
    swap = [(0, 0), (1, 2), (2, 1), (3, 3)]
    product = lax.ppermute(product, ("core", "zl"), swap)
    trace = lax.ppermute(trace, ("core", "zl"), swap)

    weights = solve(here, steer, coarse, product, trace)

    holder = np.argsort(solver_index()).tolist()
    lower = lax.ppermute(weights, PARTS, list(zip(holder[:-1], holder[1:])))
    higher = lax.ppermute(weights, PARTS, list(zip(holder[1:], holder[:-1])))
    beamed = form_beams(here, lower, weights, higher).transpose(1, 0, 2)
    turned = lax.all_to_all(beamed, PARTS, split_axis=0, concat_axis=0, tiled=True)
    inverse = fourier_matrix(FREQUENCY_BINS, 1.0).transpose(1, 0, 2, 3)[solver_index()]
    series = jnp.einsum("kps,kpqt->qst", turned, inverse, preferred_element_type=F32)
    return series.reshape(1, 2, SPECTRA * FREQUENCY_BINS)


def solution(mesh):
    fine = Mesh(mesh.devices.reshape(SIZES), PARTS)
    placed = (P(None, PARTS, None), P(PARTS, None, None, None), P(), P())
    return jax.shard_map(
        shards, mesh=fine, in_specs=placed, out_specs=P(PARTS, None, None), check_vma=False
    )
```

```python
import functools
import math

import jax
import jax.numpy as jnp
import ml_dtypes
import numpy as np
from jax import lax
from jax.experimental import pallas as pl
from jax.experimental.pallas import tpu as pltpu
from jax.sharding import Mesh
from jax.sharding import PartitionSpec as P

FREQUENCY_BINS = 128
LOAD_PCT = 10
KEEP_PCT = 50
PHASE_STEPS = 4096

PARTS = ("zh", "core", "x", "y", "zl")
SIZES = (2, 2, 4, 4, 2)
SOLVER = ("zh", "zl", "x", "y", "core")
DEVICES = 128

ANTENNAS = 2048
BEAMS = 128
SPECTRA = 384
HERE = 16
TAIL = 16
PIECES = 2
PIECE = ANTENNAS // PIECES
CHUNK = 512
COLUMNS = 256

BLOCK = 16384

BF = jnp.bfloat16
F32 = jnp.float32
ANY = pl.BlockSpec(memory_space=pl.ANY)
VMEM = pl.BlockSpec(memory_space=pltpu.VMEM)
SMEM = pl.BlockSpec(memory_space=pltpu.SMEM)


TURNED = (((1,), (1,)), ((), ()))


def solver_index():
    grid = np.arange(DEVICES).reshape(SIZES)
    return np.transpose(grid, (0, 4, 2, 3, 1)).reshape(-1)


def fourier_matrix(length, sign):
    counter = np.arange(length, dtype=np.int64)
    angle = (counter[:, None] * counter[None, :] % length) * (2.0 * math.pi / length)
    cosine = np.cos(angle) / math.sqrt(length)
    sine = sign * np.sin(angle) / math.sqrt(length)
    table = np.stack([np.stack([cosine, sine], axis=1), np.stack([-sine, cosine], axis=1)], axis=0)
    return table.astype(np.float32).astype(ml_dtypes.bfloat16)


def dot(a, b):
    return jnp.dot(a, b, preferred_element_type=F32)


def placed(space, *operands):
    return [pltpu.with_memory_space_constraint(x, space) for x in operands]


def channelize_kernel(table, voltages, out, rows, turned):
    step = BLOCK // FREQUENCY_BINS
    for p in range(2):
        for s in range(step):
            tile = voltages[p, :, s * FREQUENCY_BINS : (s + 1) * FREQUENCY_BINS]
            rows[p, s * HERE : (s + 1) * HERE] = tile.astype(F32)
    for a in range(HERE):
        mine = pl.ds(a, step, stride=HERE)
        signal = jnp.concatenate([rows[0, mine], rows[1, mine]], axis=1).astype(BF)
        spectrum = lax.dot_general(table[...], signal, TURNED, preferred_element_type=F32)
        turned[pl.ds(a, 2 * FREQUENCY_BINS, stride=HERE)] = spectrum
    out[...] = turned[...].astype(BF).reshape(FREQUENCY_BINS, 2, HERE, step)


def channelize(voltages):
    step = BLOCK // FREQUENCY_BINS
    table = fourier_matrix(FREQUENCY_BINS, -1.0)[..., solver_index()]
    table = table.transpose(3, 2, 0, 1).reshape(2 * FREQUENCY_BINS, 2 * FREQUENCY_BINS)
    return pl.pallas_call(
        channelize_kernel,
        grid=(SPECTRA // step,),
        in_specs=[
            pl.BlockSpec(table.shape, lambda j: (0, 0)),
            pl.BlockSpec((2, HERE, BLOCK), lambda j: (0, 0, j)),
        ],
        out_specs=pl.BlockSpec((FREQUENCY_BINS, 2, HERE, step), lambda j: (0, 0, 0, j)),
        out_shape=pltpu.HBM((FREQUENCY_BINS, 2, HERE, SPECTRA), BF),
        scratch_shapes=[
            pltpu.VMEM((2, step * HERE, FREQUENCY_BINS), F32),
            pltpu.VMEM((2 * FREQUENCY_BINS * HERE, step), F32),
        ],
        compiler_params=pltpu.CompilerParams(vmem_limit_bytes=40 << 20),
        name="channelize",
    )(*placed(pltpu.HBM, jnp.asarray(table), voltages))


def steering(pos, directions, channel):
    phase = ((pos * directions) & (PHASE_STEPS - 1)) * (channel + FREQUENCY_BINS)
    moved = (phase & (PHASE_STEPS - 1)) + 512
    quadrant = moved >> 10
    x = ((moved & 1023) - 512).astype(F32) * (2.0 * math.pi / PHASE_STEPS)
    y = x * x
    sine = 1.0 / 362880.0
    for c in (-1.0 / 5040.0, 1.0 / 120.0, -1.0 / 6.0, 1.0):
        sine = sine * y + c
    sine = sine * x
    cosine = 1.0 / 40320.0
    for c in (-1.0 / 720.0, 1.0 / 24.0, -0.5, 1.0):
        cosine = cosine * y + c
    odd = (quadrant & 1) == 1
    c = jnp.where(odd, sine, cosine)
    s = jnp.where(odd, cosine, sine)
    c = jnp.where(((quadrant + 1) & 2) == 2, -c, c)
    s = jnp.where((quadrant & 2) == 2, -s, s)
    return c, s


def earlier_kernel(channels, pos, directions, trace, earlier, *rest):
    product, (steer, coarse, own) = rest[:PIECES], rest[PIECES:]
    j = pl.program_id(0)

    @pl.when(j == 0)
    def _():
        for i in range(ANTENNAS // COLUMNS):
            at = slice(i * COLUMNS, (i + 1) * COLUMNS)
            c, s = steering(pos[:, at], directions[...], channels[0])
            own[:BEAMS, at] = c.astype(BF)
            own[BEAMS:, at] = s.astype(BF)

    here = pl.ds(pl.multiple_of(j * COLUMNS, COLUMNS), COLUMNS)
    c, s = steering(pos[:, here], directions[...], channels[1])
    steer[:BEAMS] = c
    steer[BEAMS:] = s
    coarse[:BEAMS] = c.astype(BF)
    coarse[BEAMS:] = s.astype(BF)
    first = dot(own[...], earlier[0, 0])
    second = dot(own[...], earlier[0, 1])
    total = jnp.sum(trace[...], keepdims=True)
    high = total.astype(BF)
    middle = (total - high.astype(F32)).astype(BF)
    low = (total - high.astype(F32) - middle.astype(F32)).astype(BF)
    row = lax.broadcasted_iota(jnp.int32, (TAIL, COLUMNS), 0)
    tail = jnp.where(row == 2, low.astype(F32), 0.0)
    tail = jnp.where(row == 1, middle.astype(F32), tail)
    tail = jnp.where(row == 0, high.astype(F32), tail).astype(BF)
    for i in range(PIECES):

        @pl.when(j // (PIECE // COLUMNS) == i)
        def _():
            product[i][:BEAMS] = (first[:BEAMS] + second[BEAMS:]).astype(BF)
            product[i][BEAMS : 2 * BEAMS] = (first[BEAMS:] - second[:BEAMS]).astype(BF)
            product[i][2 * BEAMS :] = tail


def diagonal_kernel(earlier, trace):
    @pl.when(pl.program_id(0) == 0)
    def _():
        trace[...] = jnp.zeros_like(trace)

    square = earlier[0, 0].astype(F32)
    row = lax.broadcasted_iota(jnp.int32, square.shape, 0)
    column = lax.broadcasted_iota(jnp.int32, square.shape, 1)
    kept = jnp.where(row == column, square, 0.0)
    kept = jnp.sum(kept.reshape(COLUMNS // 8, 8, COLUMNS), axis=0)
    trace[...] += kept[:, :128] + kept[:, 128:]


def diagonal(earlier):
    return pl.pallas_call(
        diagonal_kernel,
        grid=(ANTENNAS // COLUMNS,),
        in_specs=[pl.BlockSpec((1, 1, COLUMNS, COLUMNS), lambda j: (0, 0, j, j))],
        out_specs=pl.BlockSpec((8, 128), lambda j: (0, 0)),
        out_shape=jax.ShapeDtypeStruct((8, 128), F32),
        compiler_params=pltpu.CompilerParams(vmem_limit_bytes=8 << 20),
        name="diagonal",
    )(*placed(pltpu.HBM, earlier))


def piece_block(i):
    steps = PIECE // COLUMNS
    return pl.BlockSpec((2 * BEAMS + TAIL, COLUMNS), lambda j: (0, jnp.clip(j - i * steps, 0, steps - 1)))


def earlier_product(channels, pos, directions, trace, earlier):
    steps = ANTENNAS // COLUMNS
    wide = pl.BlockSpec((2 * BEAMS, COLUMNS), lambda j: (0, j))
    return pl.pallas_call(
        earlier_kernel,
        grid=(steps,),
        in_specs=[
            SMEM,
            pl.BlockSpec((1, ANTENNAS), lambda j: (0, 0)),
            pl.BlockSpec((BEAMS, 1), lambda j: (0, 0)),
            pl.BlockSpec((8, 128), lambda j: (0, 0)),
            pl.BlockSpec((1, 2, ANTENNAS, COLUMNS), lambda j: (0, 0, 0, j)),
        ],
        out_specs=[piece_block(i) for i in range(PIECES)] + [wide, wide],
        out_shape=[pltpu.HBM((2 * BEAMS + TAIL, PIECE), BF)] * PIECES
        + [
            pltpu.HBM((2 * BEAMS, ANTENNAS), F32),
            pltpu.HBM((2 * BEAMS, ANTENNAS), BF),
        ],
        scratch_shapes=[pltpu.VMEM((2 * BEAMS, ANTENNAS), BF)],
        compiler_params=pltpu.CompilerParams(vmem_limit_bytes=20 << 20),
        name="earlier_product",
    )(channels, pos, directions, trace, *placed(pltpu.HBM, earlier))


def antennas_of(here, part, chunk):
    at = pl.ds(chunk * (CHUNK // HERE), CHUNK // HERE)
    return here[at, part].reshape(CHUNK, SPECTRA)


def data_kernel(here, coarse_hbm, steer_hbm, *rest):
    data, steer, power, (coarse, sems) = rest[:PIECES], rest[PIECES : 2 * PIECES], rest[2 * PIECES], rest[2 * PIECES + 1 :]
    copies = [pltpu.make_async_copy(coarse_hbm, coarse, sems.at[0])]
    for i in range(PIECES):
        source = steer_hbm.at[:, pl.ds(i * PIECE, PIECE)]
        copies.append(pltpu.make_async_copy(source, steer[i], sems.at[1 + i]))
    for c in copies:
        c.start()
    total = jnp.zeros((8, SPECTRA), F32)
    for chunk in range(ANTENNAS // CHUNK):
        for part in range(2):
            x = antennas_of(here, part, chunk).astype(F32).reshape(CHUNK // 8, 8, SPECTRA)
            total += jnp.sum(x * x, axis=0)
    power[...] = total
    copies[0].wait()
    first = jnp.zeros((2 * BEAMS, SPECTRA), F32)
    second = jnp.zeros((2 * BEAMS, SPECTRA), F32)
    for chunk in range(ANTENNAS // CHUNK):
        at = slice(chunk * CHUNK, (chunk + 1) * CHUNK)
        first += dot(coarse[:, at], antennas_of(here, 0, chunk))
        second += dot(coarse[:, at], antennas_of(here, 1, chunk))
    inner = jnp.concatenate(
        [first[:BEAMS] + second[BEAMS:], first[BEAMS:] - second[:BEAMS]], axis=0
    ).astype(BF)
    for chunk in range(ANTENNAS // CHUNK):
        piece, offset = divmod(chunk * CHUNK, PIECE)
        at = slice(offset, offset + CHUNK)
        p = lax.dot_general(inner, antennas_of(here, 0, chunk), TURNED, preferred_element_type=F32)
        q = lax.dot_general(inner, antennas_of(here, 1, chunk), TURNED, preferred_element_type=F32)
        data[piece][:BEAMS, at] = p[:BEAMS] - q[BEAMS:]
        data[piece][BEAMS:, at] = p[BEAMS:] + q[:BEAMS]
    for c in copies[1:]:
        c.wait()


def data_product(here, coarse, steer):
    piece = pltpu.VMEM((2 * BEAMS, PIECE), F32)
    out = pl.pallas_call(
        data_kernel,
        in_specs=[VMEM, ANY, ANY],
        out_specs=[VMEM] * (2 * PIECES + 1),
        out_shape=[piece] * (2 * PIECES) + [pltpu.VMEM((8, SPECTRA), F32)],
        scratch_shapes=[pltpu.VMEM((2 * BEAMS, ANTENNAS), BF), pltpu.SemaphoreType.DMA((1 + PIECES,))],
        compiler_params=pltpu.CompilerParams(vmem_limit_bytes=12 << 20),
        name="data_product",
    )(*placed(pltpu.VMEM, here), *placed(pltpu.HBM, coarse, steer))
    return out[:PIECES], out[PIECES : 2 * PIECES], out[2 * PIECES]


def weights_kernel(data, steer, power, trace, product, out):
    keep = KEEP_PCT / 100.0
    fresh = (1.0 - keep) / SPECTRA
    total = jnp.sum(power[...], keepdims=True) * fresh + jnp.sum(trace[2 * BEAMS :, :1].astype(F32), keepdims=True) * keep
    mean_diag = total * (1.0 / ANTENNAS)
    loading = LOAD_PCT / 100.0 * mean_diag
    upper = 5.0 * mean_diag
    center = 0.5 * (upper + loading)
    radius = 0.5 * (upper - loading)
    ratio = center / radius
    factor = 1.0 / ratio
    factor_next = 1.0 / (2.0 * ratio - factor)
    beta = 2.0 * factor_next / (radius * center)
    alpha = (1.0 + factor_next * factor) / center + 2.0 * factor_next / radius
    out[...] = (
        (alpha - beta * loading) * steer[...]
        - (keep * beta) * product[: 2 * BEAMS].astype(F32)
        - (fresh * beta) * data[...]
    ).astype(BF)


def weigh(*operands):
    return pl.pallas_call(
        weights_kernel,
        in_specs=[VMEM] * 5,
        out_specs=VMEM,
        out_shape=pltpu.VMEM((2 * BEAMS, PIECE), BF),
        compiler_params=pltpu.CompilerParams(vmem_limit_bytes=8 << 20),
        name="weights",
    )(*placed(pltpu.VMEM, *operands))


def beams_kernel(piece, here, own, chip, link, *rest):
    *before, out = rest
    if before:
        first, second = before[0][0], before[0][1]
    else:
        first = jnp.zeros((2 * BEAMS, SPECTRA), F32)
        second = jnp.zeros((2 * BEAMS, SPECTRA), F32)
    for chunk in range(PIECE // CHUNK):
        at = slice(chunk * CHUNK, (chunk + 1) * CHUNK)
        smooth = (
            0.25 * (chip[:, at].astype(F32) + link[:, at].astype(F32)) + 0.5 * own[:, at].astype(F32)
        ).astype(BF)
        first += dot(smooth, antennas_of(here, 0, piece * (PIECE // CHUNK) + chunk))
        second += dot(smooth, antennas_of(here, 1, piece * (PIECE // CHUNK) + chunk))
    if piece < PIECES - 1:
        out[0] = first
        out[1] = second
    else:
        out[0] = (first[:BEAMS] + second[BEAMS:]).astype(BF)
        out[1] = (second[:BEAMS] - first[BEAMS:]).astype(BF)


def form_beams(piece, *operands):
    last = piece == PIECES - 1
    out = pltpu.VMEM((2, BEAMS, SPECTRA), BF) if last else pltpu.VMEM((2, 2 * BEAMS, SPECTRA), F32)
    return pl.pallas_call(
        functools.partial(beams_kernel, piece),
        in_specs=[VMEM] * len(operands),
        out_specs=VMEM,
        out_shape=out,
        compiler_params=pltpu.CompilerParams(vmem_limit_bytes=12 << 20),
        name="form_beams",
    )(*placed(pltpu.VMEM, *operands))


def shards(voltages, earlier, antenna_pos, beam_dir):
    spectra = channelize(voltages)
    here = lax.all_to_all(spectra, PARTS, split_axis=0, concat_axis=0, tiled=True)

    channels = jnp.stack([lax.axis_index(PARTS), lax.axis_index(SOLVER)]).astype(jnp.int32)
    *product, steer, coarse = earlier_product(
        channels,
        antenna_pos.reshape(1, ANTENNAS),
        beam_dir.reshape(BEAMS, 1),
        diagonal(earlier),
        earlier,
    )
    swap = [(0, 0), (1, 2), (2, 1), (3, 3)]
    product = [lax.ppermute(x, ("core", "zl"), swap) for x in product]
    trace = product[0]

    data, steer, power = data_product(here, coarse, steer)

    holder = np.argsort(solver_index()).tolist()
    pairs = list(zip(holder[1:-1:2], holder[2::2]))
    pairs = pairs + [(b, a) for a, b in pairs]
    sides = []
    for i in range(PIECES):
        weights = weigh(data[i], steer[i], power, trace, product[i])
        link = lax.ppermute(weights, PARTS, pairs)
        chip = lax.ppermute(weights, "core", [(0, 1), (1, 0)])
        sides.append((weights, chip, link))
    sums = ()
    for i in range(PIECES):
        sums = (form_beams(i, here, *sides[i], *sums),)
    beamed = sums[0]
    turned = lax.all_to_all(beamed.transpose(1, 0, 2), PARTS, split_axis=0, concat_axis=0, tiled=True)
    inverse = fourier_matrix(FREQUENCY_BINS, 1.0).transpose(1, 0, 2, 3)[solver_index()]
    series = jnp.einsum("kps,kpqt->qst", turned, inverse, preferred_element_type=F32)
    return series.reshape(1, 2, SPECTRA * FREQUENCY_BINS)


def solution(mesh):
    fine = Mesh(mesh.devices.reshape(SIZES), PARTS)
    placed = (P(None, PARTS, None), P(PARTS, None, None, None), P(), P())
    return jax.shard_map(
        shards, mesh=fine, in_specs=placed, out_specs=P(PARTS, None, None), check_vma=False
    )
```

```python
import functools
import math

import jax
import jax.numpy as jnp
import ml_dtypes
import numpy as np
from jax import lax
from jax.experimental import pallas as pl
from jax.experimental.pallas import tpu as pltpu
from jax.sharding import Mesh
from jax.sharding import PartitionSpec as P

FREQUENCY_BINS = 128
LOAD_PCT = 10
KEEP_PCT = 50
PHASE_STEPS = 4096

PARTS = ("zh", "core", "x", "y", "zl")
SIZES = (2, 2, 4, 4, 2)
SOLVER = ("zh", "zl", "x", "y", "core")
DEVICES = 128

ANTENNAS = 2048
BEAMS = 128
SPECTRA = 384
HERE = 16
TAIL = 16
PIECES = 2
PIECE = ANTENNAS // PIECES
CHUNK = 512
COLUMNS = 256

GROUP = 8

BF = jnp.bfloat16
F32 = jnp.float32
ANY = pl.BlockSpec(memory_space=pl.ANY)
VMEM = pl.BlockSpec(memory_space=pltpu.VMEM)
SMEM = pl.BlockSpec(memory_space=pltpu.SMEM)


TURNED = (((1,), (1,)), ((), ()))


def solver_index():
    grid = np.arange(DEVICES).reshape(SIZES)
    return np.transpose(grid, (0, 4, 2, 3, 1)).reshape(-1)


def fourier_matrix(length, sign):
    counter = np.arange(length, dtype=np.int64)
    angle = (counter[:, None] * counter[None, :] % length) * (2.0 * math.pi / length)
    cosine = np.cos(angle) / math.sqrt(length)
    sine = sign * np.sin(angle) / math.sqrt(length)
    table = np.stack([np.stack([cosine, sine], axis=1), np.stack([-sine, cosine], axis=1)], axis=0)
    return table.astype(np.float32).astype(ml_dtypes.bfloat16)


def dot(a, b):
    return jnp.dot(a, b, preferred_element_type=F32)


def placed(space, *operands):
    return [pltpu.with_memory_space_constraint(x, space) for x in operands]


def channelize_kernel(table, voltages, out, rows, turned):
    for p in range(2):
        for s in range(SPECTRA):
            tile = voltages[p, :, s * FREQUENCY_BINS : (s + 1) * FREQUENCY_BINS]
            rows[p, s * GROUP : (s + 1) * GROUP] = tile.astype(F32)
    for a in range(GROUP):
        mine = pl.ds(a, SPECTRA, stride=GROUP)
        signal = jnp.concatenate([rows[0, mine], rows[1, mine]], axis=1).astype(BF)
        spectrum = lax.dot_general(table[...], signal, TURNED, preferred_element_type=F32)
        for b in range(SPECTRA // 128):
            turned[b, pl.ds(a, 2 * FREQUENCY_BINS, stride=GROUP)] = spectrum[:, b * 128 : (b + 1) * 128]
    for b in range(SPECTRA // 128):
        block = turned[b].astype(BF).reshape(FREQUENCY_BINS, 2, GROUP, 128)
        out[:, :, :, b * 128 : (b + 1) * 128] = block


def channelize(voltages):
    table = fourier_matrix(FREQUENCY_BINS, -1.0)[..., solver_index()]
    table = table.transpose(3, 2, 0, 1).reshape(2 * FREQUENCY_BINS, 2 * FREQUENCY_BINS)
    return pl.pallas_call(
        channelize_kernel,
        grid=(HERE // GROUP,),
        in_specs=[
            pl.BlockSpec(table.shape, lambda i: (0, 0)),
            pl.BlockSpec((2, GROUP, SPECTRA * FREQUENCY_BINS), lambda i: (0, i, 0)),
        ],
        out_specs=pl.BlockSpec((FREQUENCY_BINS, 2, GROUP, SPECTRA), lambda i: (0, 0, i, 0)),
        out_shape=pltpu.HBM((FREQUENCY_BINS, 2, HERE, SPECTRA), BF),
        scratch_shapes=[
            pltpu.VMEM((2, SPECTRA * GROUP, FREQUENCY_BINS), F32),
            pltpu.VMEM((SPECTRA // 128, 2 * FREQUENCY_BINS * GROUP, 128), F32),
        ],
        compiler_params=pltpu.CompilerParams(vmem_limit_bytes=40 << 20),
        name="channelize",
    )(*placed(pltpu.HBM, jnp.asarray(table), voltages))


def steering(pos, directions, channel):
    phase = ((pos * directions) & (PHASE_STEPS - 1)) * (channel + FREQUENCY_BINS)
    moved = (phase & (PHASE_STEPS - 1)) + 512
    quadrant = moved >> 10
    x = ((moved & 1023) - 512).astype(F32) * (2.0 * math.pi / PHASE_STEPS)
    y = x * x
    sine = 1.0 / 362880.0
    for c in (-1.0 / 5040.0, 1.0 / 120.0, -1.0 / 6.0, 1.0):
        sine = sine * y + c
    sine = sine * x
    cosine = 1.0 / 40320.0
    for c in (-1.0 / 720.0, 1.0 / 24.0, -0.5, 1.0):
        cosine = cosine * y + c
    odd = (quadrant & 1) == 1
    c = jnp.where(odd, sine, cosine)
    s = jnp.where(odd, cosine, sine)
    c = jnp.where(((quadrant + 1) & 2) == 2, -c, c)
    s = jnp.where((quadrant & 2) == 2, -s, s)
    return c, s


def earlier_kernel(channels, pos, directions, trace, earlier, *rest):
    product, (steer, coarse, own) = rest[:PIECES], rest[PIECES:]
    j = pl.program_id(0)

    @pl.when(j == 0)
    def _():
        for i in range(ANTENNAS // COLUMNS):
            at = slice(i * COLUMNS, (i + 1) * COLUMNS)
            c, s = steering(pos[:, at], directions[...], channels[0])
            own[:BEAMS, at] = c.astype(BF)
            own[BEAMS:, at] = s.astype(BF)

    here = pl.ds(pl.multiple_of(j * COLUMNS, COLUMNS), COLUMNS)
    c, s = steering(pos[:, here], directions[...], channels[1])
    steer[:BEAMS] = c
    steer[BEAMS:] = s
    coarse[:BEAMS] = c.astype(BF)
    coarse[BEAMS:] = s.astype(BF)
    first = dot(own[...], earlier[0, 0])
    second = dot(own[...], earlier[0, 1])
    total = jnp.sum(trace[...], keepdims=True)
    high = total.astype(BF)
    middle = (total - high.astype(F32)).astype(BF)
    low = (total - high.astype(F32) - middle.astype(F32)).astype(BF)
    row = lax.broadcasted_iota(jnp.int32, (TAIL, COLUMNS), 0)
    tail = jnp.where(row == 2, low.astype(F32), 0.0)
    tail = jnp.where(row == 1, middle.astype(F32), tail)
    tail = jnp.where(row == 0, high.astype(F32), tail).astype(BF)
    for i in range(PIECES):

        @pl.when(j // (PIECE // COLUMNS) == i)
        def _():
            product[i][:BEAMS] = (first[:BEAMS] + second[BEAMS:]).astype(BF)
            product[i][BEAMS : 2 * BEAMS] = (first[BEAMS:] - second[:BEAMS]).astype(BF)
            product[i][2 * BEAMS :] = tail


def diagonal_kernel(earlier, trace):
    @pl.when(pl.program_id(0) == 0)
    def _():
        trace[...] = jnp.zeros_like(trace)

    square = earlier[0, 0].astype(F32)
    row = lax.broadcasted_iota(jnp.int32, square.shape, 0)
    column = lax.broadcasted_iota(jnp.int32, square.shape, 1)
    kept = jnp.where(row == column, square, 0.0)
    kept = jnp.sum(kept.reshape(COLUMNS // 8, 8, COLUMNS), axis=0)
    trace[...] += kept[:, :128] + kept[:, 128:]


def diagonal(earlier):
    return pl.pallas_call(
        diagonal_kernel,
        grid=(ANTENNAS // COLUMNS,),
        in_specs=[pl.BlockSpec((1, 1, COLUMNS, COLUMNS), lambda j: (0, 0, j, j))],
        out_specs=pl.BlockSpec((8, 128), lambda j: (0, 0)),
        out_shape=jax.ShapeDtypeStruct((8, 128), F32),
        compiler_params=pltpu.CompilerParams(vmem_limit_bytes=8 << 20),
        name="diagonal",
    )(*placed(pltpu.HBM, earlier))


def piece_block(i):
    steps = PIECE // COLUMNS
    return pl.BlockSpec((2 * BEAMS + TAIL, COLUMNS), lambda j: (0, jnp.clip(j - i * steps, 0, steps - 1)))


def earlier_product(channels, pos, directions, trace, earlier):
    steps = ANTENNAS // COLUMNS
    wide = pl.BlockSpec((2 * BEAMS, COLUMNS), lambda j: (0, j))
    return pl.pallas_call(
        earlier_kernel,
        grid=(steps,),
        in_specs=[
            SMEM,
            pl.BlockSpec((1, ANTENNAS), lambda j: (0, 0)),
            pl.BlockSpec((BEAMS, 1), lambda j: (0, 0)),
            pl.BlockSpec((8, 128), lambda j: (0, 0)),
            pl.BlockSpec((1, 2, ANTENNAS, COLUMNS), lambda j: (0, 0, 0, j)),
        ],
        out_specs=[piece_block(i) for i in range(PIECES)] + [wide, wide],
        out_shape=[pltpu.HBM((2 * BEAMS + TAIL, PIECE), BF)] * PIECES
        + [
            pltpu.HBM((2 * BEAMS, ANTENNAS), F32),
            pltpu.HBM((2 * BEAMS, ANTENNAS), BF),
        ],
        scratch_shapes=[pltpu.VMEM((2 * BEAMS, ANTENNAS), BF)],
        compiler_params=pltpu.CompilerParams(vmem_limit_bytes=20 << 20),
        name="earlier_product",
    )(channels, pos, directions, trace, *placed(pltpu.HBM, earlier))


def antennas_of(here, part, chunk):
    at = pl.ds(chunk * (CHUNK // HERE), CHUNK // HERE)
    return here[at, part].reshape(CHUNK, SPECTRA)


def data_kernel(here, coarse_hbm, steer_hbm, *rest):
    data, steer, power, (coarse, sems) = rest[:PIECES], rest[PIECES : 2 * PIECES], rest[2 * PIECES], rest[2 * PIECES + 1 :]
    copies = [pltpu.make_async_copy(coarse_hbm, coarse, sems.at[0])]
    for i in range(PIECES):
        source = steer_hbm.at[:, pl.ds(i * PIECE, PIECE)]
        copies.append(pltpu.make_async_copy(source, steer[i], sems.at[1 + i]))
    for c in copies:
        c.start()
    total = jnp.zeros((8, SPECTRA), F32)
    for chunk in range(ANTENNAS // CHUNK):
        for part in range(2):
            x = antennas_of(here, part, chunk).astype(F32).reshape(CHUNK // 8, 8, SPECTRA)
            total += jnp.sum(x * x, axis=0)
    power[...] = total
    copies[0].wait()
    first = jnp.zeros((2 * BEAMS, SPECTRA), F32)
    second = jnp.zeros((2 * BEAMS, SPECTRA), F32)
    for chunk in range(ANTENNAS // CHUNK):
        at = slice(chunk * CHUNK, (chunk + 1) * CHUNK)
        first += dot(coarse[:, at], antennas_of(here, 0, chunk))
        second += dot(coarse[:, at], antennas_of(here, 1, chunk))
    inner = jnp.concatenate(
        [first[:BEAMS] + second[BEAMS:], first[BEAMS:] - second[:BEAMS]], axis=0
    ).astype(BF)
    for chunk in range(ANTENNAS // CHUNK):
        piece, offset = divmod(chunk * CHUNK, PIECE)
        at = slice(offset, offset + CHUNK)
        p = lax.dot_general(inner, antennas_of(here, 0, chunk), TURNED, preferred_element_type=F32)
        q = lax.dot_general(inner, antennas_of(here, 1, chunk), TURNED, preferred_element_type=F32)
        data[piece][:BEAMS, at] = p[:BEAMS] - q[BEAMS:]
        data[piece][BEAMS:, at] = p[BEAMS:] + q[:BEAMS]
    for c in copies[1:]:
        c.wait()


def data_product(here, coarse, steer):
    piece = pltpu.VMEM((2 * BEAMS, PIECE), F32)
    out = pl.pallas_call(
        data_kernel,
        in_specs=[VMEM, ANY, ANY],
        out_specs=[VMEM] * (2 * PIECES + 1),
        out_shape=[piece] * (2 * PIECES) + [pltpu.VMEM((8, SPECTRA), F32)],
        scratch_shapes=[pltpu.VMEM((2 * BEAMS, ANTENNAS), BF), pltpu.SemaphoreType.DMA((1 + PIECES,))],
        compiler_params=pltpu.CompilerParams(vmem_limit_bytes=12 << 20),
        name="data_product",
    )(*placed(pltpu.VMEM, here), *placed(pltpu.HBM, coarse, steer))
    return out[:PIECES], out[PIECES : 2 * PIECES], out[2 * PIECES]


def weights_kernel(data, steer, power, trace, product, out):
    keep = KEEP_PCT / 100.0
    fresh = (1.0 - keep) / SPECTRA
    total = jnp.sum(power[...], keepdims=True) * fresh + jnp.sum(trace[2 * BEAMS :, :1].astype(F32), keepdims=True) * keep
    mean_diag = total * (1.0 / ANTENNAS)
    loading = LOAD_PCT / 100.0 * mean_diag
    upper = 5.0 * mean_diag
    center = 0.5 * (upper + loading)
    radius = 0.5 * (upper - loading)
    ratio = center / radius
    factor = 1.0 / ratio
    factor_next = 1.0 / (2.0 * ratio - factor)
    beta = 2.0 * factor_next / (radius * center)
    alpha = (1.0 + factor_next * factor) / center + 2.0 * factor_next / radius
    out[...] = (
        (alpha - beta * loading) * steer[...]
        - (keep * beta) * product[: 2 * BEAMS].astype(F32)
        - (fresh * beta) * data[...]
    ).astype(BF)


def weigh(*operands):
    return pl.pallas_call(
        weights_kernel,
        in_specs=[VMEM] * 5,
        out_specs=VMEM,
        out_shape=pltpu.VMEM((2 * BEAMS, PIECE), BF),
        compiler_params=pltpu.CompilerParams(vmem_limit_bytes=8 << 20),
        name="weights",
    )(*placed(pltpu.VMEM, *operands))


def beams_kernel(piece, here, own, chip, link, *rest):
    *before, out = rest
    if before:
        first, second = before[0][0], before[0][1]
    else:
        first = jnp.zeros((2 * BEAMS, SPECTRA), F32)
        second = jnp.zeros((2 * BEAMS, SPECTRA), F32)
    for chunk in range(PIECE // CHUNK):
        at = slice(chunk * CHUNK, (chunk + 1) * CHUNK)
        smooth = (
            0.25 * (chip[:, at].astype(F32) + link[:, at].astype(F32)) + 0.5 * own[:, at].astype(F32)
        ).astype(BF)
        first += dot(smooth, antennas_of(here, 0, piece * (PIECE // CHUNK) + chunk))
        second += dot(smooth, antennas_of(here, 1, piece * (PIECE // CHUNK) + chunk))
    if piece < PIECES - 1:
        out[0] = first
        out[1] = second
    else:
        out[0] = (first[:BEAMS] + second[BEAMS:]).astype(BF)
        out[1] = (second[:BEAMS] - first[BEAMS:]).astype(BF)


def form_beams(piece, *operands):
    last = piece == PIECES - 1
    out = pltpu.VMEM((2, BEAMS, SPECTRA), BF) if last else pltpu.VMEM((2, 2 * BEAMS, SPECTRA), F32)
    return pl.pallas_call(
        functools.partial(beams_kernel, piece),
        in_specs=[VMEM] * len(operands),
        out_specs=VMEM,
        out_shape=out,
        compiler_params=pltpu.CompilerParams(vmem_limit_bytes=12 << 20),
        name="form_beams",
    )(*placed(pltpu.VMEM, *operands))


def series_kernel(beams, inverse, out):
    series = lax.dot_general(beams[...], inverse[...], (((0,), (0,)), ((), ())), preferred_element_type=F32)
    for q in range(2):
        out[pl.ds(q, SPECTRA, stride=2)] = series[:, q * FREQUENCY_BINS : (q + 1) * FREQUENCY_BINS]


def resynthesize(beams, inverse):
    return pl.pallas_call(
        series_kernel,
        in_specs=[VMEM, VMEM],
        out_specs=VMEM,
        out_shape=jax.ShapeDtypeStruct((2 * SPECTRA, FREQUENCY_BINS), F32),
        compiler_params=pltpu.CompilerParams(vmem_limit_bytes=12 << 20),
        name="resynthesize",
    )(*placed(pltpu.VMEM, beams, inverse))


def shards(voltages, earlier, antenna_pos, beam_dir):
    spectra = channelize(voltages)
    here = lax.all_to_all(spectra, PARTS, split_axis=0, concat_axis=0, tiled=True)

    channels = jnp.stack([lax.axis_index(PARTS), lax.axis_index(SOLVER)]).astype(jnp.int32)
    *product, steer, coarse = earlier_product(
        channels,
        antenna_pos.reshape(1, ANTENNAS),
        beam_dir.reshape(BEAMS, 1),
        diagonal(earlier),
        earlier,
    )
    swap = [(0, 0), (1, 2), (2, 1), (3, 3)]
    product = [lax.ppermute(x, ("core", "zl"), swap) for x in product]
    trace = product[0]

    data, steer, power = data_product(here, coarse, steer)

    holder = np.argsort(solver_index()).tolist()
    pairs = list(zip(holder[1:-1:2], holder[2::2]))
    pairs = pairs + [(b, a) for a, b in pairs]
    sides = []
    for i in range(PIECES):
        weights = weigh(data[i], steer[i], power, trace, product[i])
        link = lax.ppermute(weights, PARTS, pairs)
        chip = lax.ppermute(weights, "core", [(0, 1), (1, 0)])
        sides.append((weights, chip, link))
    sums = ()
    for i in range(PIECES):
        sums = (form_beams(i, here, *sides[i], *sums),)
    beamed = sums[0]
    turned = lax.all_to_all(beamed.transpose(1, 0, 2), PARTS, split_axis=0, concat_axis=0, tiled=True)
    inverse = fourier_matrix(FREQUENCY_BINS, 1.0).transpose(1, 0, 2, 3)[solver_index()]
    series = resynthesize(turned.reshape(2 * FREQUENCY_BINS, SPECTRA), jnp.asarray(inverse.reshape(2 * FREQUENCY_BINS, 2 * FREQUENCY_BINS)))
    return series.reshape(SPECTRA, 2, FREQUENCY_BINS).transpose(1, 0, 2).reshape(1, 2, SPECTRA * FREQUENCY_BINS)


def solution(mesh):
    fine = Mesh(mesh.devices.reshape(SIZES), PARTS)
    placed = (P(None, PARTS, None), P(PARTS, None, None, None), P(), P())
    return jax.shard_map(
        shards, mesh=fine, in_specs=placed, out_specs=P(PARTS, None, None), check_vma=False
    )
```

```python
import functools
import math

import jax
import jax.numpy as jnp
import ml_dtypes
import numpy as np
from jax import lax
from jax.experimental import pallas as pl
from jax.experimental.pallas import tpu as pltpu
from jax.sharding import Mesh
from jax.sharding import PartitionSpec as P

FREQUENCY_BINS = 128
LOAD_PCT = 10
KEEP_PCT = 50
PHASE_STEPS = 4096

PARTS = ("zh", "core", "x", "y", "zl")
SIZES = (2, 2, 4, 4, 2)
SOLVER = ("zh", "zl", "x", "y", "core")
DEVICES = 128

ANTENNAS = 2048
BEAMS = 128
SPECTRA = 384
HERE = 16
TAIL = 16
PIECES = 2
PIECE = ANTENNAS // PIECES
CHUNK = 512
COLUMNS = 256

GROUP = 8

BF = jnp.bfloat16
F32 = jnp.float32
ANY = pl.BlockSpec(memory_space=pl.ANY)
VMEM = pl.BlockSpec(memory_space=pltpu.VMEM)
SMEM = pl.BlockSpec(memory_space=pltpu.SMEM)


TURNED = (((1,), (1,)), ((), ()))


def solver_index():
    grid = np.arange(DEVICES).reshape(SIZES)
    return np.transpose(grid, (0, 4, 2, 3, 1)).reshape(-1)


def fourier_matrix(length, sign):
    counter = np.arange(length, dtype=np.int64)
    angle = (counter[:, None] * counter[None, :] % length) * (2.0 * math.pi / length)
    cosine = np.cos(angle) / math.sqrt(length)
    sine = sign * np.sin(angle) / math.sqrt(length)
    table = np.stack([np.stack([cosine, sine], axis=1), np.stack([-sine, cosine], axis=1)], axis=0)
    return table.astype(np.float32).astype(ml_dtypes.bfloat16)


def dot(a, b):
    return jnp.dot(a, b, preferred_element_type=F32)


def placed(space, *operands):
    return [pltpu.with_memory_space_constraint(x, space) for x in operands]


def channelize_kernel(table, voltages, out, rows, turned):
    for p in range(2):
        for s in range(SPECTRA):
            tile = voltages[p, :, s * FREQUENCY_BINS : (s + 1) * FREQUENCY_BINS]
            rows[p, s * GROUP : (s + 1) * GROUP] = tile.astype(F32)
    for a in range(GROUP):
        mine = pl.ds(a, SPECTRA, stride=GROUP)
        signal = jnp.concatenate([rows[0, mine], rows[1, mine]], axis=1).astype(BF)
        spectrum = lax.dot_general(table[...], signal, TURNED, preferred_element_type=F32)
        for b in range(SPECTRA // 128):
            turned[b, pl.ds(a, 2 * FREQUENCY_BINS, stride=GROUP)] = spectrum[:, b * 128 : (b + 1) * 128]
    for b in range(SPECTRA // 128):
        block = turned[b].astype(BF).reshape(FREQUENCY_BINS, 2, GROUP, 128)
        out[:, :, :, b * 128 : (b + 1) * 128] = block


def channelize(voltages):
    table = fourier_matrix(FREQUENCY_BINS, -1.0)[..., solver_index()]
    table = table.transpose(3, 2, 0, 1).reshape(2 * FREQUENCY_BINS, 2 * FREQUENCY_BINS)
    return pl.pallas_call(
        channelize_kernel,
        grid=(HERE // GROUP,),
        in_specs=[
            pl.BlockSpec(table.shape, lambda i: (0, 0)),
            pl.BlockSpec((2, GROUP, SPECTRA * FREQUENCY_BINS), lambda i: (0, i, 0)),
        ],
        out_specs=pl.BlockSpec((FREQUENCY_BINS, 2, GROUP, SPECTRA), lambda i: (0, 0, i, 0)),
        out_shape=pltpu.HBM((FREQUENCY_BINS, 2, HERE, SPECTRA), BF),
        scratch_shapes=[
            pltpu.VMEM((2, SPECTRA * GROUP, FREQUENCY_BINS), F32),
            pltpu.VMEM((SPECTRA // 128, 2 * FREQUENCY_BINS * GROUP, 128), F32),
        ],
        compiler_params=pltpu.CompilerParams(vmem_limit_bytes=40 << 20),
        name="channelize",
    )(*placed(pltpu.HBM, jnp.asarray(table), voltages))


def steering(pos, directions, channel):
    phase = ((pos * directions) & (PHASE_STEPS - 1)) * (channel + FREQUENCY_BINS)
    moved = (phase & (PHASE_STEPS - 1)) + 512
    quadrant = moved >> 10
    x = ((moved & 1023) - 512).astype(F32) * (2.0 * math.pi / PHASE_STEPS)
    y = x * x
    sine = 1.0 / 362880.0
    for c in (-1.0 / 5040.0, 1.0 / 120.0, -1.0 / 6.0, 1.0):
        sine = sine * y + c
    sine = sine * x
    cosine = 1.0 / 40320.0
    for c in (-1.0 / 720.0, 1.0 / 24.0, -0.5, 1.0):
        cosine = cosine * y + c
    odd = (quadrant & 1) == 1
    c = jnp.where(odd, sine, cosine)
    s = jnp.where(odd, cosine, sine)
    c = jnp.where(((quadrant + 1) & 2) == 2, -c, c)
    s = jnp.where((quadrant & 2) == 2, -s, s)
    return c, s


def earlier_kernel(channels, pos, directions, trace, earlier, *rest):
    product, (steer, coarse, own) = rest[:PIECES], rest[PIECES:]
    j = pl.program_id(0)

    @pl.when(j == 0)
    def _():
        for i in range(ANTENNAS // COLUMNS):
            at = slice(i * COLUMNS, (i + 1) * COLUMNS)
            c, s = steering(pos[:, at], directions[...], channels[0])
            own[:BEAMS, at] = c.astype(BF)
            own[BEAMS:, at] = s.astype(BF)

    here = pl.ds(pl.multiple_of(j * COLUMNS, COLUMNS), COLUMNS)
    c, s = steering(pos[:, here], directions[...], channels[1])
    steer[:BEAMS] = c
    steer[BEAMS:] = s
    coarse[:BEAMS] = c.astype(BF)
    coarse[BEAMS:] = s.astype(BF)
    first = dot(own[...], earlier[0, 0])
    second = dot(own[...], earlier[0, 1])
    total = jnp.sum(trace[...], keepdims=True)
    high = total.astype(BF)
    middle = (total - high.astype(F32)).astype(BF)
    low = (total - high.astype(F32) - middle.astype(F32)).astype(BF)
    row = lax.broadcasted_iota(jnp.int32, (TAIL, COLUMNS), 0)
    tail = jnp.where(row == 2, low.astype(F32), 0.0)
    tail = jnp.where(row == 1, middle.astype(F32), tail)
    tail = jnp.where(row == 0, high.astype(F32), tail).astype(BF)
    for i in range(PIECES):

        @pl.when(j // (PIECE // COLUMNS) == i)
        def _():
            product[i][:BEAMS] = (first[:BEAMS] + second[BEAMS:]).astype(BF)
            product[i][BEAMS : 2 * BEAMS] = (first[BEAMS:] - second[:BEAMS]).astype(BF)
            product[i][2 * BEAMS :] = tail


def diagonal_kernel(earlier, trace):
    @pl.when(pl.program_id(0) == 0)
    def _():
        trace[...] = jnp.zeros_like(trace)

    square = earlier[0, 0].astype(F32)
    row = lax.broadcasted_iota(jnp.int32, square.shape, 0)
    column = lax.broadcasted_iota(jnp.int32, square.shape, 1)
    kept = jnp.where(row == column, square, 0.0)
    kept = jnp.sum(kept.reshape(COLUMNS // 8, 8, COLUMNS), axis=0)
    trace[...] += kept[:, :128] + kept[:, 128:]


def diagonal(earlier):
    return pl.pallas_call(
        diagonal_kernel,
        grid=(ANTENNAS // COLUMNS,),
        in_specs=[pl.BlockSpec((1, 1, COLUMNS, COLUMNS), lambda j: (0, 0, j, j))],
        out_specs=pl.BlockSpec((8, 128), lambda j: (0, 0)),
        out_shape=jax.ShapeDtypeStruct((8, 128), F32),
        compiler_params=pltpu.CompilerParams(vmem_limit_bytes=8 << 20),
        name="diagonal",
    )(*placed(pltpu.HBM, earlier))


def piece_block(i):
    steps = PIECE // COLUMNS
    return pl.BlockSpec((2 * BEAMS + TAIL, COLUMNS), lambda j: (0, jnp.clip(j - i * steps, 0, steps - 1)))


def earlier_product(channels, pos, directions, trace, earlier):
    steps = ANTENNAS // COLUMNS
    wide = pl.BlockSpec((2 * BEAMS, COLUMNS), lambda j: (0, j))
    return pl.pallas_call(
        earlier_kernel,
        grid=(steps,),
        in_specs=[
            SMEM,
            pl.BlockSpec((1, ANTENNAS), lambda j: (0, 0)),
            pl.BlockSpec((BEAMS, 1), lambda j: (0, 0)),
            pl.BlockSpec((8, 128), lambda j: (0, 0)),
            pl.BlockSpec((1, 2, ANTENNAS, COLUMNS), lambda j: (0, 0, 0, j)),
        ],
        out_specs=[piece_block(i) for i in range(PIECES)] + [wide, wide],
        out_shape=[pltpu.HBM((2 * BEAMS + TAIL, PIECE), BF)] * PIECES
        + [
            pltpu.HBM((2 * BEAMS, ANTENNAS), F32),
            pltpu.HBM((2 * BEAMS, ANTENNAS), BF),
        ],
        scratch_shapes=[pltpu.VMEM((2 * BEAMS, ANTENNAS), BF)],
        compiler_params=pltpu.CompilerParams(vmem_limit_bytes=20 << 20),
        name="earlier_product",
    )(channels, pos, directions, trace, *placed(pltpu.HBM, earlier))


def antennas_of(here, part, chunk):
    at = pl.ds(chunk * (CHUNK // HERE), CHUNK // HERE)
    return here[at, part].reshape(CHUNK, SPECTRA)


def data_kernel(here, coarse_hbm, steer_hbm, *rest):
    data, steer, power, (coarse, sems) = rest[:PIECES], rest[PIECES : 2 * PIECES], rest[2 * PIECES], rest[2 * PIECES + 1 :]
    copies = [pltpu.make_async_copy(coarse_hbm, coarse, sems.at[0])]
    for i in range(PIECES):
        source = steer_hbm.at[:, pl.ds(i * PIECE, PIECE)]
        copies.append(pltpu.make_async_copy(source, steer[i], sems.at[1 + i]))
    for c in copies:
        c.start()
    total = jnp.zeros((8, SPECTRA), F32)
    for chunk in range(ANTENNAS // CHUNK):
        for part in range(2):
            x = antennas_of(here, part, chunk).astype(F32).reshape(CHUNK // 8, 8, SPECTRA)
            total += jnp.sum(x * x, axis=0)
    power[...] = total
    copies[0].wait()
    first = jnp.zeros((2 * BEAMS, SPECTRA), F32)
    second = jnp.zeros((2 * BEAMS, SPECTRA), F32)
    for chunk in range(ANTENNAS // CHUNK):
        at = slice(chunk * CHUNK, (chunk + 1) * CHUNK)
        first += dot(coarse[:, at], antennas_of(here, 0, chunk))
        second += dot(coarse[:, at], antennas_of(here, 1, chunk))
    inner = jnp.concatenate(
        [first[:BEAMS] + second[BEAMS:], first[BEAMS:] - second[:BEAMS]], axis=0
    ).astype(BF)
    for chunk in range(ANTENNAS // CHUNK):
        piece, offset = divmod(chunk * CHUNK, PIECE)
        at = slice(offset, offset + CHUNK)
        p = lax.dot_general(inner, antennas_of(here, 0, chunk), TURNED, preferred_element_type=F32)
        q = lax.dot_general(inner, antennas_of(here, 1, chunk), TURNED, preferred_element_type=F32)
        data[piece][:BEAMS, at] = p[:BEAMS] - q[BEAMS:]
        data[piece][BEAMS:, at] = p[BEAMS:] + q[:BEAMS]
    for c in copies[1:]:
        c.wait()


def data_product(here, coarse, steer):
    piece = pltpu.VMEM((2 * BEAMS, PIECE), F32)
    out = pl.pallas_call(
        data_kernel,
        in_specs=[VMEM, ANY, ANY],
        out_specs=[VMEM] * (2 * PIECES + 1),
        out_shape=[piece] * (2 * PIECES) + [pltpu.VMEM((8, SPECTRA), F32)],
        scratch_shapes=[pltpu.VMEM((2 * BEAMS, ANTENNAS), BF), pltpu.SemaphoreType.DMA((1 + PIECES,))],
        compiler_params=pltpu.CompilerParams(vmem_limit_bytes=12 << 20),
        name="data_product",
    )(*placed(pltpu.VMEM, here), *placed(pltpu.HBM, coarse, steer))
    return out[:PIECES], out[PIECES : 2 * PIECES], out[2 * PIECES]


def weights_kernel(data, steer, power, trace_hbm, product_hbm, out, trace, product, sems):
    copies = [
        pltpu.make_async_copy(trace_hbm.at[pl.ds(2 * BEAMS, TAIL), pl.ds(0, 128)], trace, sems.at[0]),
        pltpu.make_async_copy(product_hbm.at[pl.ds(0, 2 * BEAMS)], product, sems.at[1]),
    ]
    for c in copies:
        c.start()
    copies[0].wait()
    keep = KEEP_PCT / 100.0
    fresh = (1.0 - keep) / SPECTRA
    total = jnp.sum(power[...], keepdims=True) * fresh + jnp.sum(trace[:, :1].astype(F32), keepdims=True) * keep
    mean_diag = total * (1.0 / ANTENNAS)
    loading = LOAD_PCT / 100.0 * mean_diag
    upper = 5.0 * mean_diag
    center = 0.5 * (upper + loading)
    radius = 0.5 * (upper - loading)
    ratio = center / radius
    factor = 1.0 / ratio
    factor_next = 1.0 / (2.0 * ratio - factor)
    beta = 2.0 * factor_next / (radius * center)
    alpha = (1.0 + factor_next * factor) / center + 2.0 * factor_next / radius
    copies[1].wait()
    out[...] = (
        (alpha - beta * loading) * steer[...]
        - (keep * beta) * product[...].astype(F32)
        - (fresh * beta) * data[...]
    ).astype(BF)


def weigh(data, steer, power, trace, product):
    return pl.pallas_call(
        weights_kernel,
        in_specs=[VMEM, VMEM, VMEM, ANY, ANY],
        out_specs=VMEM,
        out_shape=pltpu.VMEM((2 * BEAMS, PIECE), BF),
        scratch_shapes=[
            pltpu.VMEM((TAIL, 128), BF),
            pltpu.VMEM((2 * BEAMS, PIECE), BF),
            pltpu.SemaphoreType.DMA((2,)),
        ],
        compiler_params=pltpu.CompilerParams(vmem_limit_bytes=8 << 20),
        name="weights",
    )(*placed(pltpu.VMEM, data, steer, power), *placed(pltpu.HBM, trace, product))


def beams_kernel(piece, here, own, chip, link, *rest):
    *before, out = rest
    if before:
        first, second = before[0][0], before[0][1]
    else:
        first = jnp.zeros((2 * BEAMS, SPECTRA), F32)
        second = jnp.zeros((2 * BEAMS, SPECTRA), F32)
    for chunk in range(PIECE // CHUNK):
        at = slice(chunk * CHUNK, (chunk + 1) * CHUNK)
        smooth = (
            0.25 * (chip[:, at].astype(F32) + link[:, at].astype(F32)) + 0.5 * own[:, at].astype(F32)
        ).astype(BF)
        first += dot(smooth, antennas_of(here, 0, piece * (PIECE // CHUNK) + chunk))
        second += dot(smooth, antennas_of(here, 1, piece * (PIECE // CHUNK) + chunk))
    if piece < PIECES - 1:
        out[0] = first
        out[1] = second
    else:
        out[0] = (first[:BEAMS] + second[BEAMS:]).astype(BF)
        out[1] = (second[:BEAMS] - first[BEAMS:]).astype(BF)


def form_beams(piece, *operands):
    last = piece == PIECES - 1
    out = pltpu.VMEM((2, BEAMS, SPECTRA), BF) if last else pltpu.VMEM((2, 2 * BEAMS, SPECTRA), F32)
    return pl.pallas_call(
        functools.partial(beams_kernel, piece),
        in_specs=[VMEM] * len(operands),
        out_specs=VMEM,
        out_shape=out,
        compiler_params=pltpu.CompilerParams(vmem_limit_bytes=12 << 20),
        name="form_beams",
    )(*placed(pltpu.VMEM, *operands))


def series_kernel(beams, inverse, out):
    series = lax.dot_general(beams[...], inverse[...], (((0,), (0,)), ((), ())), preferred_element_type=F32)
    for q in range(2):
        out[pl.ds(q, SPECTRA, stride=2)] = series[:, q * FREQUENCY_BINS : (q + 1) * FREQUENCY_BINS]


def resynthesize(beams, inverse):
    return pl.pallas_call(
        series_kernel,
        in_specs=[VMEM, VMEM],
        out_specs=VMEM,
        out_shape=jax.ShapeDtypeStruct((2 * SPECTRA, FREQUENCY_BINS), F32),
        compiler_params=pltpu.CompilerParams(vmem_limit_bytes=12 << 20),
        name="resynthesize",
    )(*placed(pltpu.VMEM, beams, inverse))


def shards(voltages, earlier, antenna_pos, beam_dir):
    spectra = channelize(voltages)
    here = lax.all_to_all(spectra, PARTS, split_axis=0, concat_axis=0, tiled=True)

    channels = jnp.stack([lax.axis_index(PARTS), lax.axis_index(SOLVER)]).astype(jnp.int32)
    *product, steer, coarse = earlier_product(
        channels,
        antenna_pos.reshape(1, ANTENNAS),
        beam_dir.reshape(BEAMS, 1),
        diagonal(earlier),
        earlier,
    )
    swap = [(0, 0), (1, 2), (2, 1), (3, 3)]
    product = [lax.ppermute(x, ("core", "zl"), swap) for x in product]
    trace = product[0]

    data, steer, power = data_product(here, coarse, steer)

    holder = np.argsort(solver_index()).tolist()
    pairs = list(zip(holder[1:-1:2], holder[2::2]))
    pairs = pairs + [(b, a) for a, b in pairs]
    sides = []
    for i in range(PIECES):
        weights = weigh(data[i], steer[i], power, trace, product[i])
        link = lax.ppermute(weights, PARTS, pairs)
        chip = lax.ppermute(weights, "core", [(0, 1), (1, 0)])
        sides.append((weights, chip, link))
    sums = ()
    for i in range(PIECES):
        sums = (form_beams(i, here, *sides[i], *sums),)
    beamed = sums[0]
    turned = lax.all_to_all(beamed.transpose(1, 0, 2), PARTS, split_axis=0, concat_axis=0, tiled=True)
    inverse = fourier_matrix(FREQUENCY_BINS, 1.0).transpose(1, 0, 2, 3)[solver_index()]
    series = resynthesize(turned.reshape(2 * FREQUENCY_BINS, SPECTRA), jnp.asarray(inverse.reshape(2 * FREQUENCY_BINS, 2 * FREQUENCY_BINS)))
    return series.reshape(SPECTRA, 2, FREQUENCY_BINS).transpose(1, 0, 2).reshape(1, 2, SPECTRA * FREQUENCY_BINS)


def solution(mesh):
    fine = Mesh(mesh.devices.reshape(SIZES), PARTS)
    placed = (P(None, PARTS, None), P(PARTS, None, None, None), P(), P())
    return jax.shard_map(
        shards, mesh=fine, in_specs=placed, out_specs=P(PARTS, None, None), check_vma=False
    )
```

```python
import functools
import math

import jax
import jax.numpy as jnp
import ml_dtypes
import numpy as np
from jax import lax
from jax.experimental import pallas as pl
from jax.experimental.pallas import tpu as pltpu
from jax.sharding import Mesh
from jax.sharding import PartitionSpec as P

FREQUENCY_BINS = 128
LOAD_PCT = 10
KEEP_PCT = 50
PHASE_STEPS = 4096

PARTS = ("zh", "core", "x", "y", "zl")
SIZES = (2, 2, 4, 4, 2)
SOLVER = ("zh", "zl", "x", "y", "core")
DEVICES = 128

ANTENNAS = 2048
BEAMS = 128
SPECTRA = 384
HERE = 16
TAIL = 16
PIECES = 2
PIECE = ANTENNAS // PIECES
CHUNK = 512
COLUMNS = 256

GROUP = 8

BF = jnp.bfloat16
F32 = jnp.float32
ANY = pl.BlockSpec(memory_space=pl.ANY)
VMEM = pl.BlockSpec(memory_space=pltpu.VMEM)
SMEM = pl.BlockSpec(memory_space=pltpu.SMEM)


TURNED = (((1,), (1,)), ((), ()))


def solver_index():
    grid = np.arange(DEVICES).reshape(SIZES)
    return np.transpose(grid, (0, 4, 2, 3, 1)).reshape(-1)


def fourier_matrix(length, sign):
    counter = np.arange(length, dtype=np.int64)
    angle = (counter[:, None] * counter[None, :] % length) * (2.0 * math.pi / length)
    cosine = np.cos(angle) / math.sqrt(length)
    sine = sign * np.sin(angle) / math.sqrt(length)
    table = np.stack([np.stack([cosine, sine], axis=1), np.stack([-sine, cosine], axis=1)], axis=0)
    return table.astype(np.float32).astype(ml_dtypes.bfloat16)


def dot(a, b):
    return jnp.dot(a, b, preferred_element_type=F32)


def placed(space, *operands):
    return [pltpu.with_memory_space_constraint(x, space) for x in operands]


def channelize_kernel(table, voltages, out, rows, turned):
    for p in range(2):
        for s in range(SPECTRA):
            tile = voltages[p, :, s * FREQUENCY_BINS : (s + 1) * FREQUENCY_BINS]
            rows[p, s * GROUP : (s + 1) * GROUP] = tile.astype(F32)
    for a in range(GROUP):
        mine = pl.ds(a, SPECTRA, stride=GROUP)
        signal = jnp.concatenate([rows[0, mine], rows[1, mine]], axis=1).astype(BF)
        spectrum = lax.dot_general(table[...], signal, TURNED, preferred_element_type=F32)
        for b in range(SPECTRA // 128):
            turned[b, pl.ds(a, 2 * FREQUENCY_BINS, stride=GROUP)] = spectrum[:, b * 128 : (b + 1) * 128]
    for b in range(SPECTRA // 128):
        block = turned[b].astype(BF).reshape(FREQUENCY_BINS, 2, GROUP, 128)
        out[:, :, :, b * 128 : (b + 1) * 128] = block


def channelize(voltages):
    table = fourier_matrix(FREQUENCY_BINS, -1.0)[..., solver_index()]
    table = table.transpose(3, 2, 0, 1).reshape(2 * FREQUENCY_BINS, 2 * FREQUENCY_BINS)
    return pl.pallas_call(
        channelize_kernel,
        grid=(HERE // GROUP,),
        in_specs=[
            pl.BlockSpec(table.shape, lambda i: (0, 0)),
            pl.BlockSpec((2, GROUP, SPECTRA * FREQUENCY_BINS), lambda i: (0, i, 0)),
        ],
        out_specs=pl.BlockSpec((FREQUENCY_BINS, 2, GROUP, SPECTRA), lambda i: (0, 0, i, 0)),
        out_shape=pltpu.HBM((FREQUENCY_BINS, 2, HERE, SPECTRA), BF),
        scratch_shapes=[
            pltpu.VMEM((2, SPECTRA * GROUP, FREQUENCY_BINS), F32),
            pltpu.VMEM((SPECTRA // 128, 2 * FREQUENCY_BINS * GROUP, 128), F32),
        ],
        compiler_params=pltpu.CompilerParams(vmem_limit_bytes=40 << 20),
        name="channelize",
    )(*placed(pltpu.HBM, jnp.asarray(table), voltages))


def steering(pos, directions, channel):
    phase = ((pos * directions) & (PHASE_STEPS - 1)) * (channel + FREQUENCY_BINS)
    moved = (phase & (PHASE_STEPS - 1)) + 512
    quadrant = moved >> 10
    x = ((moved & 1023) - 512).astype(F32) * (2.0 * math.pi / PHASE_STEPS)
    y = x * x
    sine = 1.0 / 362880.0
    for c in (-1.0 / 5040.0, 1.0 / 120.0, -1.0 / 6.0, 1.0):
        sine = sine * y + c
    sine = sine * x
    cosine = 1.0 / 40320.0
    for c in (-1.0 / 720.0, 1.0 / 24.0, -0.5, 1.0):
        cosine = cosine * y + c
    odd = (quadrant & 1) == 1
    c = jnp.where(odd, sine, cosine)
    s = jnp.where(odd, cosine, sine)
    c = jnp.where(((quadrant + 1) & 2) == 2, -c, c)
    s = jnp.where((quadrant & 2) == 2, -s, s)
    return c, s


def earlier_kernel(channels, pos, directions, trace, earlier, *rest):
    product, (steer, coarse, own) = rest[:PIECES], rest[PIECES:]
    j = pl.program_id(0)

    @pl.when(j == 0)
    def _():
        for i in range(ANTENNAS // COLUMNS):
            at = slice(i * COLUMNS, (i + 1) * COLUMNS)
            c, s = steering(pos[:, at], directions[...], channels[0])
            own[:BEAMS, at] = c.astype(BF)
            own[BEAMS:, at] = s.astype(BF)

    here = pl.ds(pl.multiple_of(j * COLUMNS, COLUMNS), COLUMNS)
    c, s = steering(pos[:, here], directions[...], channels[1])
    steer[:BEAMS] = c
    steer[BEAMS:] = s
    coarse[:BEAMS] = c.astype(BF)
    coarse[BEAMS:] = s.astype(BF)
    first = dot(own[...], earlier[0, 0])
    second = dot(own[...], earlier[0, 1])
    total = jnp.sum(trace[...], keepdims=True)
    high = total.astype(BF)
    middle = (total - high.astype(F32)).astype(BF)
    low = (total - high.astype(F32) - middle.astype(F32)).astype(BF)
    row = lax.broadcasted_iota(jnp.int32, (TAIL, COLUMNS), 0)
    tail = jnp.where(row == 2, low.astype(F32), 0.0)
    tail = jnp.where(row == 1, middle.astype(F32), tail)
    tail = jnp.where(row == 0, high.astype(F32), tail).astype(BF)
    for i in range(PIECES):

        @pl.when(j // (PIECE // COLUMNS) == i)
        def _():
            product[i][:BEAMS] = (first[:BEAMS] + second[BEAMS:]).astype(BF)
            product[i][BEAMS : 2 * BEAMS] = (first[BEAMS:] - second[:BEAMS]).astype(BF)
            product[i][2 * BEAMS :] = tail


def diagonal_kernel(earlier, trace):
    @pl.when(pl.program_id(0) == 0)
    def _():
        trace[...] = jnp.zeros_like(trace)

    square = earlier[0, 0].astype(F32)
    row = lax.broadcasted_iota(jnp.int32, square.shape, 0)
    column = lax.broadcasted_iota(jnp.int32, square.shape, 1)
    kept = jnp.where(row == column, square, 0.0)
    kept = jnp.sum(kept.reshape(COLUMNS // 8, 8, COLUMNS), axis=0)
    trace[...] += kept[:, :128] + kept[:, 128:]


def diagonal(earlier):
    return pl.pallas_call(
        diagonal_kernel,
        grid=(ANTENNAS // COLUMNS,),
        in_specs=[pl.BlockSpec((1, 1, COLUMNS, COLUMNS), lambda j: (0, 0, j, j))],
        out_specs=pl.BlockSpec((8, 128), lambda j: (0, 0)),
        out_shape=jax.ShapeDtypeStruct((8, 128), F32),
        compiler_params=pltpu.CompilerParams(vmem_limit_bytes=8 << 20),
        name="diagonal",
    )(*placed(pltpu.HBM, earlier))


def piece_block(i):
    steps = PIECE // COLUMNS
    return pl.BlockSpec((2 * BEAMS + TAIL, COLUMNS), lambda j: (0, jnp.clip(j - i * steps, 0, steps - 1)))


def earlier_product(channels, pos, directions, trace, earlier):
    steps = ANTENNAS // COLUMNS
    wide = pl.BlockSpec((2 * BEAMS, COLUMNS), lambda j: (0, j))
    return pl.pallas_call(
        earlier_kernel,
        grid=(steps,),
        in_specs=[
            SMEM,
            pl.BlockSpec((1, ANTENNAS), lambda j: (0, 0)),
            pl.BlockSpec((BEAMS, 1), lambda j: (0, 0)),
            pl.BlockSpec((8, 128), lambda j: (0, 0)),
            pl.BlockSpec((1, 2, ANTENNAS, COLUMNS), lambda j: (0, 0, 0, j)),
        ],
        out_specs=[piece_block(i) for i in range(PIECES)] + [wide, wide],
        out_shape=[pltpu.HBM((2 * BEAMS + TAIL, PIECE), BF)] * PIECES
        + [
            pltpu.HBM((2 * BEAMS, ANTENNAS), F32),
            pltpu.HBM((2 * BEAMS, ANTENNAS), BF),
        ],
        scratch_shapes=[pltpu.VMEM((2 * BEAMS, ANTENNAS), BF)],
        compiler_params=pltpu.CompilerParams(vmem_limit_bytes=20 << 20),
        name="earlier_product",
    )(channels, pos, directions, trace, *placed(pltpu.HBM, earlier))


def antennas_of(here, part, chunk):
    at = pl.ds(chunk * (CHUNK // HERE), CHUNK // HERE)
    return here[at, part].reshape(CHUNK, SPECTRA)


def data_kernel(here, coarse_hbm, steer_hbm, *rest):
    data, steer, power, (coarse, sems) = rest[:PIECES], rest[PIECES : 2 * PIECES], rest[2 * PIECES], rest[2 * PIECES + 1 :]
    copies = [pltpu.make_async_copy(coarse_hbm, coarse, sems.at[0])]
    for i in range(PIECES):
        source = steer_hbm.at[:, pl.ds(i * PIECE, PIECE)]
        copies.append(pltpu.make_async_copy(source, steer[i], sems.at[1 + i]))
    for c in copies:
        c.start()
    total = jnp.zeros((8, SPECTRA), F32)

    def squares(chunk):
        parts = [antennas_of(here, part, chunk).astype(F32) for part in range(2)]
        return sum(jnp.sum((x * x).reshape(CHUNK // 8, 8, SPECTRA), axis=0) for x in parts)

    early = ANTENNAS // CHUNK // 2
    for chunk in range(early):
        total += squares(chunk)
    copies[0].wait()
    first = jnp.zeros((2 * BEAMS, SPECTRA), F32)
    second = jnp.zeros((2 * BEAMS, SPECTRA), F32)
    for chunk in range(ANTENNAS // CHUNK):
        at = slice(chunk * CHUNK, (chunk + 1) * CHUNK)
        first += dot(coarse[:, at], antennas_of(here, 0, chunk))
        second += dot(coarse[:, at], antennas_of(here, 1, chunk))
        if chunk >= early:
            total += squares(chunk)
    power[...] = total
    inner = jnp.concatenate(
        [first[:BEAMS] + second[BEAMS:], first[BEAMS:] - second[:BEAMS]], axis=0
    ).astype(BF)
    for chunk in range(ANTENNAS // CHUNK):
        piece, offset = divmod(chunk * CHUNK, PIECE)
        at = slice(offset, offset + CHUNK)
        p = lax.dot_general(inner, antennas_of(here, 0, chunk), TURNED, preferred_element_type=F32)
        q = lax.dot_general(inner, antennas_of(here, 1, chunk), TURNED, preferred_element_type=F32)
        data[piece][:BEAMS, at] = p[:BEAMS] - q[BEAMS:]
        data[piece][BEAMS:, at] = p[BEAMS:] + q[:BEAMS]
    for c in copies[1:]:
        c.wait()


def data_product(here, coarse, steer):
    piece = pltpu.VMEM((2 * BEAMS, PIECE), F32)
    out = pl.pallas_call(
        data_kernel,
        in_specs=[VMEM, ANY, ANY],
        out_specs=[VMEM] * (2 * PIECES + 1),
        out_shape=[piece] * (2 * PIECES) + [pltpu.VMEM((8, SPECTRA), F32)],
        scratch_shapes=[pltpu.VMEM((2 * BEAMS, ANTENNAS), BF), pltpu.SemaphoreType.DMA((1 + PIECES,))],
        compiler_params=pltpu.CompilerParams(vmem_limit_bytes=12 << 20),
        name="data_product",
    )(*placed(pltpu.VMEM, here), *placed(pltpu.HBM, coarse, steer))
    return out[:PIECES], out[PIECES : 2 * PIECES], out[2 * PIECES]


def weights_kernel(data, steer, power, trace_hbm, product_hbm, out, trace, product, sems):
    copies = [
        pltpu.make_async_copy(trace_hbm.at[pl.ds(2 * BEAMS, TAIL), pl.ds(0, 128)], trace, sems.at[0]),
        pltpu.make_async_copy(product_hbm.at[pl.ds(0, 2 * BEAMS)], product, sems.at[1]),
    ]
    for c in copies:
        c.start()
    copies[0].wait()
    keep = KEEP_PCT / 100.0
    fresh = (1.0 - keep) / SPECTRA
    total = jnp.sum(power[...], keepdims=True) * fresh + jnp.sum(trace[:, :1].astype(F32), keepdims=True) * keep
    mean_diag = total * (1.0 / ANTENNAS)
    loading = LOAD_PCT / 100.0 * mean_diag
    upper = 5.0 * mean_diag
    center = 0.5 * (upper + loading)
    radius = 0.5 * (upper - loading)
    ratio = center / radius
    factor = 1.0 / ratio
    factor_next = 1.0 / (2.0 * ratio - factor)
    beta = 2.0 * factor_next / (radius * center)
    alpha = (1.0 + factor_next * factor) / center + 2.0 * factor_next / radius
    copies[1].wait()
    out[...] = (
        (alpha - beta * loading) * steer[...]
        - (keep * beta) * product[...].astype(F32)
        - (fresh * beta) * data[...]
    ).astype(BF)


def weigh(data, steer, power, trace, product):
    return pl.pallas_call(
        weights_kernel,
        in_specs=[VMEM, VMEM, VMEM, ANY, ANY],
        out_specs=VMEM,
        out_shape=pltpu.VMEM((2 * BEAMS, PIECE), BF),
        scratch_shapes=[
            pltpu.VMEM((TAIL, 128), BF),
            pltpu.VMEM((2 * BEAMS, PIECE), BF),
            pltpu.SemaphoreType.DMA((2,)),
        ],
        compiler_params=pltpu.CompilerParams(vmem_limit_bytes=8 << 20),
        name="weights",
    )(*placed(pltpu.VMEM, data, steer, power), *placed(pltpu.HBM, trace, product))


def beams_kernel(piece, here, own, chip, link, *rest):
    *before, out = rest
    if before:
        first, second = before[0][0], before[0][1]
    else:
        first = jnp.zeros((2 * BEAMS, SPECTRA), F32)
        second = jnp.zeros((2 * BEAMS, SPECTRA), F32)
    for chunk in range(PIECE // CHUNK):
        at = slice(chunk * CHUNK, (chunk + 1) * CHUNK)
        smooth = (
            0.25 * (chip[:, at].astype(F32) + link[:, at].astype(F32)) + 0.5 * own[:, at].astype(F32)
        ).astype(BF)
        first += dot(smooth, antennas_of(here, 0, piece * (PIECE // CHUNK) + chunk))
        second += dot(smooth, antennas_of(here, 1, piece * (PIECE // CHUNK) + chunk))
    if piece < PIECES - 1:
        out[0] = first
        out[1] = second
    else:
        out[0] = (first[:BEAMS] + second[BEAMS:]).astype(BF)
        out[1] = (second[:BEAMS] - first[BEAMS:]).astype(BF)


def form_beams(piece, *operands):
    last = piece == PIECES - 1
    out = pltpu.VMEM((2, BEAMS, SPECTRA), BF) if last else pltpu.VMEM((2, 2 * BEAMS, SPECTRA), F32)
    return pl.pallas_call(
        functools.partial(beams_kernel, piece),
        in_specs=[VMEM] * len(operands),
        out_specs=VMEM,
        out_shape=out,
        compiler_params=pltpu.CompilerParams(vmem_limit_bytes=12 << 20),
        name="form_beams",
    )(*placed(pltpu.VMEM, *operands))


def series_kernel(beams, inverse, out):
    series = lax.dot_general(beams[...], inverse[...], (((0,), (0,)), ((), ())), preferred_element_type=F32)
    for q in range(2):
        out[pl.ds(q, SPECTRA, stride=2)] = series[:, q * FREQUENCY_BINS : (q + 1) * FREQUENCY_BINS]


def resynthesize(beams, inverse):
    return pl.pallas_call(
        series_kernel,
        in_specs=[VMEM, VMEM],
        out_specs=VMEM,
        out_shape=jax.ShapeDtypeStruct((2 * SPECTRA, FREQUENCY_BINS), F32),
        compiler_params=pltpu.CompilerParams(vmem_limit_bytes=12 << 20),
        name="resynthesize",
    )(*placed(pltpu.VMEM, beams, inverse))


def shards(voltages, earlier, antenna_pos, beam_dir):
    spectra = channelize(voltages)
    here = lax.all_to_all(spectra, PARTS, split_axis=0, concat_axis=0, tiled=True)

    channels = jnp.stack([lax.axis_index(PARTS), lax.axis_index(SOLVER)]).astype(jnp.int32)
    *product, steer, coarse = earlier_product(
        channels,
        antenna_pos.reshape(1, ANTENNAS),
        beam_dir.reshape(BEAMS, 1),
        diagonal(earlier),
        earlier,
    )
    swap = [(0, 0), (1, 2), (2, 1), (3, 3)]
    product = [lax.ppermute(x, ("core", "zl"), swap) for x in product]
    trace = product[0]

    data, steer, power = data_product(here, coarse, steer)

    holder = np.argsort(solver_index()).tolist()
    pairs = list(zip(holder[1:-1:2], holder[2::2]))
    pairs = pairs + [(b, a) for a, b in pairs]
    sides = []
    for i in range(PIECES):
        weights = weigh(data[i], steer[i], power, trace, product[i])
        link = lax.ppermute(weights, PARTS, pairs)
        chip = lax.ppermute(weights, "core", [(0, 1), (1, 0)])
        sides.append((weights, chip, link))
    sums = ()
    for i in range(PIECES):
        sums = (form_beams(i, here, *sides[i], *sums),)
    beamed = sums[0]
    turned = lax.all_to_all(beamed.transpose(1, 0, 2), PARTS, split_axis=0, concat_axis=0, tiled=True)
    inverse = fourier_matrix(FREQUENCY_BINS, 1.0).transpose(1, 0, 2, 3)[solver_index()]
    series = resynthesize(turned.reshape(2 * FREQUENCY_BINS, SPECTRA), jnp.asarray(inverse.reshape(2 * FREQUENCY_BINS, 2 * FREQUENCY_BINS)))
    return series.reshape(SPECTRA, 2, FREQUENCY_BINS).transpose(1, 0, 2).reshape(1, 2, SPECTRA * FREQUENCY_BINS)


def solution(mesh):
    fine = Mesh(mesh.devices.reshape(SIZES), PARTS)
    placed = (P(None, PARTS, None), P(PARTS, None, None, None), P(), P())
    return jax.shard_map(
        shards, mesh=fine, in_specs=placed, out_specs=P(PARTS, None, None), check_vma=False
    )
```
